32 devices in a mesh: grp: 4 (over y, x), row: 8 (over z, core).
Axes of the slice: x: 2, y: 2, z: 4, core: 2. Of those that a mesh axis runs over, the one named last changes fastest.
Arguments:
- cov_prior: float32 [16384, 16384], P(('grp', 'row')), may hold values from -7 to 23, as said below
- courant_x_field: float32 [128, 128], replicated, may hold values from -0.35 to 0.35
- courant_y_field: float32 [128, 128], replicated, may hold values from -0.35 to 0.35
- obs_cells: int32 [2, 128], replicated, may hold values from 0 to 16383
- obs_var: float32 [2, 128], replicated, may hold values from 0.5 to 2
Outputs:
- analysis: float32 [16384, 16384], P('grp', 'row')
The draws below stay inside these ranges and needn't reach their ends.
Inputs may be any that keep to these rules, and one draw needn't show every extreme that they name: `cov_prior`: symmetric and positive definite. `obs_cells`: a cell may be observed more than once in an update.
All inputs are finite; a program needn't handle non-finite values.
Results may differ from the reference program's by a relative error of at most 0.0002.
Values sent between devices are 32-bit elements; how exact they have to be, the bound alone decides.
No kernel may reach another device: no remote copies, remote signals or barrier semaphores. Data moves between devices by JAX's collectives and lax.ppermute only.
A program may use at most 448 MiB of HBM per device.

```python
import math
import jax
import jax.numpy as jnp
from jax import lax

ZONAL_POINTS = 128
NY = 128
NCELL = 16384
OBS = 128
UPDATES = 2
STEPS = 1


def draw_cov_prior(key, part):
    noise_key = jax.random.fold_in(key, 101)
    scale_key = jax.random.fold_in(key, 102)
    factor_key = jax.random.fold_in(key, 103)
    factor_count = 256
    cell_ids = jnp.arange(NCELL, dtype=jnp.int32)
    column_x = cell_ids % ZONAL_POINTS
    row_y = cell_ids // ZONAL_POINTS
    offsets = [(0, 1), (0, 2), (0, 3)] + [(shift_y, shift_x) for shift_y in (1, 2, 3) for shift_x in range(-3, 4)]
    band_noise = jax.random.uniform(noise_key, (len(offsets), NCELL), jnp.float32, -0.02, 0.02)
    scales = jnp.exp(jax.random.uniform(scale_key, (NCELL,), jnp.float32, 0.0, math.log(2.0)))
    loadings = jax.random.uniform(factor_key, (NCELL, factor_count), jnp.float32, -math.sqrt(3.0), math.sqrt(3.0))
    matrix = jnp.eye(NCELL, dtype=jnp.float32)
    for position, (shift_y, shift_x) in enumerate(offsets):
        inside = (column_x + shift_x >= 0) & (column_x + shift_x < ZONAL_POINTS) & (row_y + shift_y < NY)
        target = jnp.where(inside, cell_ids + shift_y * ZONAL_POINTS + shift_x, cell_ids)
        amount = jnp.where(inside, band_noise[position], 0.0)
        matrix = matrix.at[cell_ids, target].add(amount)
        matrix = matrix.at[target, cell_ids].add(amount)
    shared = jnp.dot(loadings, loadings.T, precision=lax.Precision.HIGHEST) * (0.5 / factor_count)
    matrix = matrix + shared
    return matrix * scales[:, None] * scales[None, :]


def place_ends(values, rng, least, largest):
    dims = values.shape
    place = [jax.random.randint(jax.random.fold_in(rng, axis), (), 0, dims[axis]) for axis in range(len(dims))]
    values = values.at[tuple(place)].set(least)
    longest = dims.index(max(dims))
    place[longest] = (place[longest] + 1) % dims[longest]
    return values.at[tuple(place)].set(largest)


def setup_inputs(seed: int = 0) -> dict:
    key_of = jax.random.split(jax.random.key(seed), 6)
    cov_prior = draw_cov_prior(jax.random.fold_in(key_of[5], 71), 0)
    courant_x_field = jnp.clip(jax.random.uniform(key_of[1], (NY, ZONAL_POINTS), jnp.float32, -0.35, 0.35), -0.35, 0.35)
    courant_y_field = jnp.clip(jax.random.uniform(key_of[2], (NY, ZONAL_POINTS), jnp.float32, -0.35, 0.35), -0.35, 0.35)
    obs_cells = place_ends(jax.random.randint(key_of[3], (UPDATES, OBS), 0, NCELL), jax.random.fold_in(key_of[3], 1), 0, NCELL - 1).astype(jnp.int32)
    obs_var = jnp.clip(jnp.exp(jax.random.uniform(key_of[4], (UPDATES, OBS), jnp.float32, math.log(0.5), math.log(2.0))), 0.5, 2.0)
    return {"cov_prior": cov_prior, "courant_x_field": courant_x_field, "courant_y_field": courant_y_field, "obs_cells": obs_cells, "obs_var": obs_var}


diffusion = 0.1

def tendency(padded, u_part, v_part):
    middle = padded[:, 2:-2]
    center = middle[:, :, 2:-2]
    along_x = (8.0 * (middle[:, :, 3:-1] - middle[:, :, 1:-3]) - (middle[:, :, 4:] - middle[:, :, :-4])) / 12.0
    column = padded[:, :, 2:-2]
    along_y = (8.0 * (column[:, 3:-1] - column[:, 1:-3]) - (column[:, 4:] - column[:, :-4])) / 12.0
    laplace = middle[:, :, 3:-1] + middle[:, :, 1:-3] + column[:, 3:-1] + column[:, 1:-3] - 4.0 * center
    return diffusion * laplace - u_part * along_x - v_part * along_y

def heun_step(fields, courant_x_field, courant_y_field):
    slope_first = tendency(jnp.pad(fields, ((0, 0), (2, 2), (2, 2))), courant_x_field, courant_y_field)
    latter_increment = tendency(jnp.pad(fields + slope_first, ((0, 0), (2, 2), (2, 2))), courant_x_field, courant_y_field)
    return fields + 0.5 * (slope_first + latter_increment)

def propagate(matrix, courant_x_field, courant_y_field):
    row_count = matrix.shape[0]
    meridional_count = min(512, row_count)

    def advance_block(stacked):
        for repeat in range(STEPS):
            stacked = heun_step(stacked, courant_x_field, courant_y_field)
        return stacked
    blocks = matrix.reshape(row_count // meridional_count, meridional_count, NY, ZONAL_POINTS)
    return lax.map(advance_block, blocks).reshape(row_count, NCELL)

def reference(cov_prior, courant_x_field, courant_y_field, obs_cells, obs_var):
    advanced = propagate(cov_prior, courant_x_field, courant_y_field)
    posterior_mean = propagate(advanced.T, courant_x_field, courant_y_field).T
    for update_number in range(UPDATES):
        picked = obs_cells[update_number]
        observed_rows = posterior_mean[picked, :]
        observed_cols = posterior_mean[:, picked]
        inner_block = observed_rows[:, picked]
        system = 0.5 * (inner_block + inner_block.T) + jnp.diag(obs_var[update_number])
        factor = jnp.linalg.cholesky(system)
        halfway = lax.linalg.triangular_solve(factor, observed_rows, left_side=True, lower=True)
        weights = lax.linalg.triangular_solve(factor, halfway, left_side=True, lower=True, transpose_a=True)
        posterior_mean = posterior_mean - jnp.dot(observed_cols, weights, precision=lax.Precision.HIGHEST)
    return posterior_mean
```

```python
import functools

import jax
import jax.numpy as jnp
from jax import lax
from jax.experimental import pallas as pl
from jax.experimental.pallas import tpu as pltpu
from jax.sharding import PartitionSpec as P


diffusion = 0.1
LANES = 128
SUB = 8
REACH = 2
EXACT = lax.Precision.HIGHEST


def stencil_coefficients(u, v):
    nx = u.shape[1]
    x = lax.broadcasted_iota(jnp.int32, u.shape, 1)
    u12, v12 = u / 12.0, v / 12.0
    return [
        diffusion - 8.0 * v12,
        diffusion + 8.0 * v12,
        v12,
        jnp.where(x < nx - 1, diffusion - 8.0 * u12, 0.0),
        jnp.where(x >= 1, diffusion + 8.0 * u12, 0.0),
        jnp.where(x < nx - 2, u12, 0.0),
        jnp.where(x >= 2, -u12, 0.0),
    ]


KEEP = 1.0 - 4.0 * diffusion


def neighbours(c, ym2, ym1, yp1, yp2, xp1, xm1, xp2, xm2):
    along_y = c[0] * yp1 + c[1] * ym1 + c[2] * (yp2 - ym2)
    return along_y + ((c[3] * xp1 + c[4] * xm1) + (c[5] * xp2 + c[6] * xm2))


def row_coefficients(coefs):
    moved = [jnp.roll(c, 2, axis=1) if i in (3, 5) else c for i, c in enumerate(coefs)]
    return jnp.stack([jnp.repeat(c, SUB, axis=0) for c in moved])


def row_step_kernel(me_ref, coef_ref, p_ref, o_ref, *, nx, per_dest, lead, groups):
    me = me_ref[0]
    rows = p_ref.shape[0]
    members = o_ref.shape[0]
    depth = o_ref.shape[2] // nx
    deep = min(4, depth)
    zero = jnp.zeros((SUB, nx), jnp.float32)

    def block(step, _):
        r0 = pl.multiple_of(step * (SUB * groups), SUB * groups)

        def cols(y):
            start = y * nx
            return pl.ds(start if isinstance(start, int) else pl.multiple_of(start, nx), nx)

        def coefs(y):
            start = y * SUB
            start = start if isinstance(start, int) else pl.multiple_of(start, SUB)
            return [coef_ref[i, pl.ds(start, SUB), :] for i in range(7)]

        def around(c, m2, m1, mid, p1, p2):
            before = pltpu.roll(mid, 1, 1)
            along_y = c[0] * p1 + c[1] * m1 + c[2] * (p2 - m2)
            ahead = pltpu.roll(c[5] * mid + c[3] * before, nx - 2, 1)
            return along_y + (ahead + (c[4] * before + c[6] * pltpu.roll(before, 1, 1)))

        def part(dest, inner, low, high):
            y0 = dest * per_dest + lead + inner
            q = {}
            for k in range(-4, deep + 4):
                outside = (low and k < 0) or (high and k >= deep)
                for g in range(groups):
                    spot = pl.ds(pl.multiple_of(r0 + SUB * g, SUB), SUB)
                    q[k, g] = zero if outside else p_ref[spot, cols(y0 + k)]
            s = {}
            for k in range(-2, deep + 2):
                outside = (low and k < 0) or (high and k >= deep)
                c = None if outside else coefs(y0 + k)
                for g in range(groups):
                    s[k, g] = zero if outside else KEEP * q[k, g] + around(
                        c, *[q[k + j, g] for j in range(-2, 3)]
                    )
            slot = jnp.bitwise_xor(jnp.int32(dest), me)
            for k in range(deep):
                c = coefs(y0 + k)
                for g in range(groups):
                    value = KEEP * s[k, g] + around(c, *[s[k + j, g] for j in range(-2, 3)])
                    spot = pl.ds(pl.multiple_of(r0 + SUB * g, SUB), SUB)
                    o_ref[slot, spot, cols(inner + k)] = 0.5 * (q[k, g] + value)

        for inner in range(0, depth, deep):
            low = lead + inner == 0
            high = lead + inner + deep == per_dest
            if low:
                part(0, inner, True, high and members == 1)

            def one(dest, _):
                part(dest, inner, False, False)
                return 0

            lax.fori_loop(int(low), members - int(high), one, 0)
            if high and not (low and members == 1):
                part(members - 1, inner, False, True)
        return 0

    lax.fori_loop(0, rows // (SUB * groups), block, 0)


def row_step(cov, table, me, nx, members, lead, depth):
    rows, cells = cov.shape
    per_dest = cells // members // nx
    tall = min(64, rows)
    groups = 2 if tall % (2 * SUB) == 0 else 1
    return pl.pallas_call(
        functools.partial(row_step_kernel, nx=nx, per_dest=per_dest, lead=lead, groups=groups),
        out_shape=jax.ShapeDtypeStruct((members, rows, depth * nx), jnp.float32),
        grid_spec=pltpu.PrefetchScalarGridSpec(
            num_scalar_prefetch=1,
            grid=(rows // tall,),
            in_specs=[
                pl.BlockSpec(table.shape, lambda i, m: (0, 0, 0), pipeline_mode=pl.Buffered(1)),
                pl.BlockSpec((tall, cells), lambda i, m: (i, 0)),
            ],
            out_specs=pl.BlockSpec((members, tall, depth * nx), lambda i, m: (0, i, 0)),
        ),
        compiler_params=pltpu.CompilerParams(vmem_limit_bytes=56 << 20),
        cost_estimate=work(members * rows * depth * nx, 60),
        name="row_step",
    )(me, table, cov)


def work(elements, flops):
    return pl.CostEstimate(
        flops=flops * elements, transcendentals=0, bytes_accessed=32 * elements
    )


def pick_columns(blocks, leads, cells, me, zonal):
    total = 0.0
    for array, lead in zip(blocks, leads):
        members, _, width = array.shape
        for s in range(members):
            first = jnp.bitwise_xor(me, s) * zonal + lead
            ids = first + lax.broadcasted_iota(jnp.int32, (width, cells.shape[0]), 0)
            chosen = (ids == cells[None, :]).astype(jnp.float32)
            total = total + jnp.dot(array[s], chosen, precision=lax.Precision.HIGH)
    return total


FRONT = SUB


def column_step_kernel(me_ref, *refs, sources, halo, nx, grid_rows, update):
    coef_ref, refs = refs[0], refs[1:]
    own = refs[: len(sources)]
    refs = refs[len(sources) :]
    if update:
        c_ref, w_ref = refs[:2]
        refs = refs[2:]
        if len(refs) == 4:
            refs = refs[1:]
    o_ref, q_ref, s_ref = refs
    me = me_ref[0]
    tiles = o_ref.shape[1] // LANES
    border = jnp.zeros((FRONT, LANES), jnp.float32)
    span = (grid_rows + 4 * REACH) * nx
    for t in range(tiles):
        for ref in (q_ref, s_ref):
            ref[t, 0:FRONT, :] = border
            ref[t, FRONT + span : FRONT + span + SUB, :] = border

    for ref, (kind, at) in zip(own, sources):
        tall = ref.shape[0]
        if kind == "partner":
            start = FRONT + halo + jnp.bitwise_xor(me, at) * tall
        else:
            start = FRONT + at
        start = pl.multiple_of(start, SUB)
        piece = min(64, tall)

        def copy(i, _):
            r = pl.multiple_of(i * piece, piece)
            for t in range(tiles):
                q_ref[t, pl.ds(start + r, piece), :] = ref[
                    pl.ds(r, piece), t * LANES : (t + 1) * LANES
                ]
            return 0

        lax.fori_loop(0, tall // piece, copy, 0)

    def sweep(src, low, count, emit):
        def strip(xg, _):
            base = FRONT + xg * SUB

            def at(y, shift=0):
                rows = y * nx + base
                if shift == 0:
                    rows = pl.multiple_of(rows, SUB)
                else:
                    rows = rows + shift
                return [src[t, pl.ds(rows, SUB), :] for t in range(tiles)]

            def step(y, win):
                far = at(y + 2)
                xp1, xm1, xp2, xm2 = at(y, 1), at(y, -1), at(y, 2), at(y, -2)
                spot = pl.multiple_of(y * nx + xg * SUB, SUB)
                c = [coef_ref[i, pl.ds(spot, SUB), :] for i in range(7)]
                for t in range(tiles):
                    value = neighbours(
                        c, win[0][t], win[1][t], win[3][t], far[t],
                        xp1[t], xm1[t], xp2[t], xm2[t],
                    )
                    emit(t, spot, KEEP * win[2][t] + value)
                return win[1:] + [far]

            def several(i, win):
                for k in range(4):
                    win = step(low + 4 * i + k, win)
                return win

            win = [at(low - 2), at(low - 1), at(low), at(low + 1)]
            lax.fori_loop(0, count // 4, several, win)
            return 0

        lax.fori_loop(0, nx // SUB, strip, 0)

    def emit_first(t, spot, value):
        s_ref[t, pl.ds(spot + FRONT, SUB), :] = value

    def emit_last(t, spot, value):
        row = pl.multiple_of(spot - 2 * REACH * nx, SUB)
        mid = q_ref[t, pl.ds(pl.multiple_of(spot + FRONT, SUB), SUB), :]
        o_ref[pl.ds(row, SUB), t * LANES : (t + 1) * LANES] = 0.5 * (mid + value)

    sweep(q_ref, REACH, grid_rows + 2 * REACH, emit_first)
    sweep(s_ref, 2 * REACH, grid_rows, emit_last)

    if update:

        def subtract(y, _):
            rows = pl.ds(pl.multiple_of(y * nx, nx), nx)
            o_ref[rows, :] = o_ref[rows, :] - jnp.dot(
                c_ref[rows, :], w_ref[...], preferred_element_type=jnp.float32
            )
            return 0

        lax.fori_loop(0, grid_rows, subtract, 0)


def column_step(me, coefs, parts, sources, halo, nx, grid_rows, tile, out_shape, offset,
                own=0, gains=None, into=None):
    width = parts[0].shape[-1]
    steps = width // tile
    lead = offset // tile
    once = pl.Buffered(1)
    specs = [pl.BlockSpec(coefs.shape, lambda j, m: (0, 0, 0), pipeline_mode=once)]
    for part in parts:
        if part.ndim == 3:
            specs.append(
                pl.BlockSpec((None, part.shape[1], tile), lambda j, m: (0, 0, own // tile + j))
            )
        else:
            specs.append(pl.BlockSpec((part.shape[0], tile), lambda j, m: (0, j)))
    args = [coefs, *parts]
    aliases = {}
    if gains is not None:
        c, w = gains
        specs.append(pl.BlockSpec(c.shape, lambda j, m: (0, 0), pipeline_mode=once))
        specs.append(pl.BlockSpec((w.shape[0], tile), lambda j, m: (0, lead + j)))
        args += [c, w]
    if into is not None:
        specs.append(pl.BlockSpec(memory_space=pl.ANY))
        args.append(into)
        aliases = {len(args): 0}
    span = (grid_rows + 4 * REACH) * nx + FRONT + SUB
    scratch = pltpu.VMEM((tile // LANES, span, LANES), jnp.float32)
    return pl.pallas_call(
        functools.partial(
            column_step_kernel, sources=sources, halo=halo, nx=nx, grid_rows=grid_rows,
            update=gains is not None,
        ),
        out_shape=jax.ShapeDtypeStruct(out_shape, jnp.float32),
        grid_spec=pltpu.PrefetchScalarGridSpec(
            num_scalar_prefetch=1,
            grid=(steps,),
            in_specs=specs,
            out_specs=pl.BlockSpec((out_shape[0], tile), lambda j, m: (0, lead + j)),
            scratch_shapes=[scratch, scratch],
        ),
        input_output_aliases=aliases,
        compiler_params=pltpu.CompilerParams(vmem_limit_bytes=60 << 20),
        cost_estimate=work(out_shape[0] * width, 100),
        name="column_step",
    )(me, *args)


def split(value):
    high = lax.reduce_precision(value, 8, 7)
    return high.astype(jnp.bfloat16), (value - high).astype(jnp.bfloat16)


def solve(inner, variance, right):
    system = 0.5 * (inner + inner.T) + jnp.diag(variance)
    factor = jnp.linalg.cholesky(system)
    halfway = lax.linalg.triangular_solve(factor, right, left_side=True, lower=True)
    return lax.linalg.triangular_solve(factor, halfway, left_side=True, lower=True, transpose_a=True)


def gains_of(columns, rows, inner, obs_var):
    updates, count = obs_var.shape
    weights = []
    for u in range(updates):
        here = slice(u * count, (u + 1) * count)
        after = slice((u + 1) * count, updates * count)
        later = inner[here, after]
        both = jnp.concatenate([rows[here], later], axis=1)
        both = solve(inner[here, here], obs_var[u], both)
        w, w_later = both[:, : rows.shape[1]], both[:, rows.shape[1] :]
        weights.append(w)
        if u + 1 < updates:
            left = inner[after, here]
            rows = rows.at[after].add(-jnp.dot(left, w, precision=EXACT))
            columns = columns.at[:, after].add(-jnp.dot(columns[:, here], w_later, precision=EXACT))
            inner = inner.at[after, after].add(-jnp.dot(left, w_later, precision=EXACT))
    c_high, c_low = split(columns)
    w_high, w_low = split(jnp.concatenate(weights, axis=0))
    return (
        jnp.concatenate([c_high, c_high, c_low], axis=1),
        jnp.concatenate([w_high, w_low, w_high], axis=0),
    )


def local(cov_prior, courant_x_field, courant_y_field, obs_cells, obs_var):
    rows, cells = cov_prior.shape
    _, nx = courant_x_field.shape
    members, clusters = lax.axis_size("row"), lax.axis_size("grp")
    zonal, local_rows = cells // members, rows * members
    grid_rows = local_rows // nx
    halo = 2 * REACH * nx
    me, group = lax.axis_index("row"), lax.axis_index("grp")
    me_arg = me.reshape(1).astype(jnp.int32)
    coefs = stencil_coefficients(courant_x_field, courant_y_field)

    per_dest = zonal // nx
    table = row_coefficients(coefs)
    shares, slots = plan(per_dest)
    leads = [sum(shares[:i]) for i in range(len(shares))]
    blocks = []
    for lead, depth in zip(leads, shares):
        blocks.append(row_step(cov_prior, table, me_arg, nx, members, lead, depth))

    column_coefs = jnp.stack(
        [
            jnp.broadcast_to(
                lax.dynamic_slice_in_dim(
                    jnp.pad(c, ((2 * REACH, 2 * REACH), (0, 0))),
                    group * grid_rows, grid_rows + 4 * REACH, 0,
                ).reshape(-1)[:, None],
                (local_rows + 2 * halo, LANES),
            )
            for c in coefs
        ]
    )

    forward = [(i, i + 1) for i in range(clusters - 1)]
    backward = [(i + 1, i) for i in range(clusters - 1)]
    received = []
    for index, start, take in slots:
        cut = slice(start * nx, (start + take) * nx)
        got = [blocks[index][0, :, cut]]
        for s in range(1, members):
            pairs = [(i, i ^ s) for i in range(members)]
            got.append(lax.ppermute(blocks[index][s, :, cut], "row", pairs))
        received.append(got)

    all_cells = obs_cells.reshape(-1)
    picked = pick_columns(blocks, tuple(n * nx for n in leads), all_cells, me, zonal)
    picked = lax.all_gather(picked, "row", axis=0, tiled=True)
    below = lax.ppermute(picked[local_rows - halo :], "grp", forward)
    above = lax.ppermute(picked[:halo], "grp", backward)
    picked = jnp.concatenate([below, picked, above], axis=0)
    count = all_cells.shape[0]
    columns = column_step(
        me_arg, column_coefs, [picked], [("fixed", 0)], halo, nx, grid_rows,
        min(256, count), (local_rows, count), 0,
    )
    first_mine = me * zonal
    mine = lax.dynamic_slice_in_dim(columns, first_mine % local_rows, zonal, 0)
    mine = jnp.where(group == first_mine // local_rows, mine, 0.0)
    place = all_cells - group * local_rows
    held = (place >= 0) & (place < local_rows)
    inner = jnp.where(held[:, None], columns[jnp.clip(place, 0, local_rows - 1)], 0.0)
    mine, inner = lax.psum((mine, inner), "grp")
    gains = gains_of(columns, mine.T, inner, obs_var)

    edge = halo // rows
    result = None
    for k, (index, start, take) in enumerate(slots):
        got = received[k]
        if result is not None:
            got, result = lax.optimization_barrier((got, result))
        last = [lax.select_n(jnp.bitwise_xor(me, members - edge + i), *got) for i in range(edge)]
        head = [lax.select_n(jnp.bitwise_xor(me, i), *got) for i in range(edge)]
        below = lax.ppermute(jnp.concatenate(last, axis=0), "grp", forward)
        above = lax.ppermute(jnp.concatenate(head, axis=0), "grp", backward)
        parts = [below, above, blocks[index]] + got[1:]
        sources = [("fixed", 0), ("fixed", halo + local_rows), ("partner", 0)]
        sources += [("partner", s) for s in range(1, members)]
        result = column_step(
            me_arg, column_coefs, parts, tuple(sources), halo, nx, grid_rows,
            min(256, take * nx), (local_rows, zonal), (leads[index] + start) * nx,
            start * nx, gains, result,
        )
    return result


def plan(per_dest):
    shares = [per_dest] if per_dest <= 4 else [4, per_dest - 4]
    slots = []
    for index, depth in enumerate(shares):
        done = 0
        while done < depth:
            take = min(4, depth - done)
            if index > 0 and depth - done <= 4:
                take = min(2, depth - done)
            slots.append((index, done, take))
            done += take
    return shares, slots


def solution(mesh):
    placed = (P(("grp", "row"), None), P(), P(), P(), P())

    return jax.shard_map(
        local, mesh=mesh, in_specs=placed, out_specs=P("grp", "row"), check_vma=False
    )
```

```python
import functools

import jax
import jax.numpy as jnp
from jax import lax
from jax.experimental import pallas as pl
from jax.experimental.pallas import tpu as pltpu
from jax.sharding import PartitionSpec as P


diffusion = 0.1
LANES = 128
SUB = 8
REACH = 2
EXACT = lax.Precision.HIGHEST


def stencil_coefficients(u, v):
    nx = u.shape[1]
    x = lax.broadcasted_iota(jnp.int32, u.shape, 1)
    u12, v12 = u / 12.0, v / 12.0
    return [
        diffusion - 8.0 * v12,
        diffusion + 8.0 * v12,
        v12,
        jnp.where(x < nx - 1, diffusion - 8.0 * u12, 0.0),
        jnp.where(x >= 1, diffusion + 8.0 * u12, 0.0),
        jnp.where(x < nx - 2, u12, 0.0),
        jnp.where(x >= 2, -u12, 0.0),
    ]


KEEP = 1.0 - 4.0 * diffusion


def neighbours(c, ym2, ym1, yp1, yp2, xp1, xm1, xp2, xm2):
    along_y = c[0] * yp1 + c[1] * ym1 + c[2] * (yp2 - ym2)
    return along_y + ((c[3] * xp1 + c[4] * xm1) + (c[5] * xp2 + c[6] * xm2))


def difference_matrix(nx):
    gap = lax.broadcasted_iota(jnp.int32, (nx, nx), 0) - lax.broadcasted_iota(jnp.int32, (nx, nx), 1)
    sign = jnp.sign(gap).astype(jnp.float32)
    near, next_near = jnp.abs(gap) == 1, jnp.abs(gap) == 2
    slope = jnp.where(near, 8.0 * sign, jnp.where(next_near, -sign, 0.0))
    around = jnp.where(near, 1.0, jnp.where(gap == 0, KEEP_TENTHS, 0.0))
    once = jnp.concatenate([slope, around], axis=1)
    return jnp.concatenate([once, once], axis=0).astype(jnp.bfloat16)


KEEP_TENTHS = 6.0


def row_step_kernel(
    me_ref, coef_ref, d_ref, p_ref, o_ref, lhs_ref, ds_ref, s_ref, *, nx, per_dest, lead
):
    me = me_ref[0]
    tall = p_ref.shape[0]
    members = o_ref.shape[0]
    depth = o_ref.shape[2] // nx
    zero = jnp.zeros((tall, nx), jnp.float32)

    def at(k):
        return slice((k + 2) * tall, (k + 3) * tall)

    def put(k, value):
        high = value.astype(jnp.bfloat16)
        lhs_ref[at(k), 0:nx] = high
        lhs_ref[at(k), nx : 2 * nx] = (value - high.astype(jnp.float32)).astype(jnp.bfloat16)

    def product(k0, k1):
        rows = slice((k0 + 2) * tall, (k1 + 2) * tall)
        ds_ref[rows, :] = jnp.dot(
            lhs_ref[rows, :], d_ref[...], preferred_element_type=jnp.float32
        )

    def part(dest, low, high):
        y0 = dest * per_dest + lead

        def outside(k):
            return (low and k < 0) or (high and k >= depth)

        def cols(y):
            start = y * nx
            return pl.ds(start if isinstance(start, int) else pl.multiple_of(start, nx), nx)

        def q(k):
            return zero if outside(k) else p_ref[:, cols(y0 + k)]

        def tendency(k, m2, m1, p1, p2):
            c = [coef_ref[i, pl.ds(y0 + k, 1), :] for i in range(4)]
            along_y = (c[0] * p1 + c[1] * m1) + c[2] * (p2 - m2)
            return along_y + (diffusion * ds_ref[at(k), nx : 2 * nx] - c[3] * ds_ref[at(k), 0:nx])

        inside = [k for k in range(-2, depth + 2) if not outside(k)]
        for k in inside:
            put(k, q(k))
        product(inside[0], inside[-1] + 1)
        for k in range(-2, depth + 2):
            if outside(k):
                s_ref[at(k), :] = zero
                continue
            value = tendency(k, q(k - 2), q(k - 1), q(k + 1), q(k + 2))
            s_ref[at(k), :] = value
            if 0 <= k < depth:
                put(k, value)
        product(0, depth)
        slot = jnp.bitwise_xor(jnp.int32(dest), me)
        for k in range(depth):
            value = tendency(
                k, s_ref[at(k - 2), :], s_ref[at(k - 1), :], s_ref[at(k + 1), :], s_ref[at(k + 2), :]
            )
            o_ref[slot, :, k * nx : (k + 1) * nx] = 0.5 * (q(k) + value)

    low, high = lead == 0, lead + depth == per_dest
    if low:
        part(0, True, high and members == 1)

    def one(dest, _):
        part(dest, False, False)
        return 0

    lax.fori_loop(int(low), members - int(high), one, 0)
    if high and not (low and members == 1):
        part(members - 1, False, True)


def row_step(cov, coefs, me, nx, members, lead, depth):
    rows, cells = cov.shape
    per_dest = cells // members // nx
    tall = min(64, rows)
    table = jnp.stack(coefs)
    matrix = difference_matrix(nx)
    once = pl.Buffered(1)
    stack = (depth + 4) * tall
    return pl.pallas_call(
        functools.partial(row_step_kernel, nx=nx, per_dest=per_dest, lead=lead),
        out_shape=jax.ShapeDtypeStruct((members, rows, depth * nx), jnp.float32),
        grid_spec=pltpu.PrefetchScalarGridSpec(
            num_scalar_prefetch=1,
            grid=(rows // tall,),
            in_specs=[
                pl.BlockSpec(table.shape, lambda i, m: (0, 0, 0), pipeline_mode=once),
                pl.BlockSpec(matrix.shape, lambda i, m: (0, 0), pipeline_mode=once),
                pl.BlockSpec((tall, cells), lambda i, m: (i, 0)),
            ],
            out_specs=pl.BlockSpec((members, tall, depth * nx), lambda i, m: (0, i, 0)),
            scratch_shapes=[
                pltpu.VMEM((stack, 2 * nx), jnp.bfloat16),
                pltpu.VMEM((stack, 2 * nx), jnp.float32),
                pltpu.VMEM((stack, nx), jnp.float32),
            ],
        ),
        compiler_params=pltpu.CompilerParams(vmem_limit_bytes=56 << 20),
        cost_estimate=work(members * rows * depth * nx, 60),
        name="row_step",
    )(me, table, matrix, cov)


def work(elements, flops):
    return pl.CostEstimate(
        flops=flops * elements, transcendentals=0, bytes_accessed=32 * elements
    )


def pick_columns(blocks, leads, cells, me, zonal):
    total = 0.0
    for array, lead in zip(blocks, leads):
        members, _, width = array.shape
        for s in range(members):
            first = jnp.bitwise_xor(me, s) * zonal + lead
            ids = first + lax.broadcasted_iota(jnp.int32, (width, cells.shape[0]), 0)
            chosen = (ids == cells[None, :]).astype(jnp.float32)
            total = total + jnp.dot(array[s], chosen, precision=lax.Precision.HIGH)
    return total


FRONT = SUB


def column_step_kernel(me_ref, *refs, sources, halo, nx, grid_rows, update):
    coef_ref, refs = refs[0], refs[1:]
    own = refs[: len(sources)]
    refs = refs[len(sources) :]
    if update:
        c_ref, w_ref = refs[:2]
        refs = refs[2:]
        if len(refs) == 4:
            refs = refs[1:]
    o_ref, q_ref, s_ref = refs
    me = me_ref[0]
    tiles = o_ref.shape[1] // LANES
    border = jnp.zeros((FRONT, LANES), jnp.float32)
    span = (grid_rows + 4 * REACH) * nx
    for t in range(tiles):
        for ref in (q_ref, s_ref):
            ref[t, 0:FRONT, :] = border
            ref[t, FRONT + span : FRONT + span + SUB, :] = border

    for ref, (kind, at) in zip(own, sources):
        tall = ref.shape[0]
        if kind == "partner":
            start = FRONT + halo + jnp.bitwise_xor(me, at) * tall
        else:
            start = FRONT + at
        start = pl.multiple_of(start, SUB)
        piece = min(64, tall)

        def copy(i, _):
            r = pl.multiple_of(i * piece, piece)
            for t in range(tiles):
                q_ref[t, pl.ds(start + r, piece), :] = ref[
                    pl.ds(r, piece), t * LANES : (t + 1) * LANES
                ]
            return 0

        lax.fori_loop(0, tall // piece, copy, 0)

    def sweep(src, low, count, emit):
        def strip(xg, _):
            base = FRONT + xg * SUB

            def at(y, shift=0):
                rows = y * nx + base
                if shift == 0:
                    rows = pl.multiple_of(rows, SUB)
                else:
                    rows = rows + shift
                return [src[t, pl.ds(rows, SUB), :] for t in range(tiles)]

            def step(y, win):
                far = at(y + 2)
                xp1, xm1, xp2, xm2 = at(y, 1), at(y, -1), at(y, 2), at(y, -2)
                spot = pl.multiple_of(y * nx + xg * SUB, SUB)
                c = [coef_ref[i, pl.ds(spot, SUB), :] for i in range(7)]
                for t in range(tiles):
                    value = neighbours(
                        c, win[0][t], win[1][t], win[3][t], far[t],
                        xp1[t], xm1[t], xp2[t], xm2[t],
                    )
                    emit(t, spot, KEEP * win[2][t] + value)
                return win[1:] + [far]

            def several(i, win):
                for k in range(4):
                    win = step(low + 4 * i + k, win)
                return win

            win = [at(low - 2), at(low - 1), at(low), at(low + 1)]
            lax.fori_loop(0, count // 4, several, win)
            return 0

        lax.fori_loop(0, nx // SUB, strip, 0)

    def emit_first(t, spot, value):
        s_ref[t, pl.ds(spot + FRONT, SUB), :] = value

    def emit_last(t, spot, value):
        row = pl.multiple_of(spot - 2 * REACH * nx, SUB)
        mid = q_ref[t, pl.ds(pl.multiple_of(spot + FRONT, SUB), SUB), :]
        o_ref[pl.ds(row, SUB), t * LANES : (t + 1) * LANES] = 0.5 * (mid + value)

    sweep(q_ref, REACH, grid_rows + 2 * REACH, emit_first)
    sweep(s_ref, 2 * REACH, grid_rows, emit_last)

    if update:

        def subtract(y, _):
            rows = pl.ds(pl.multiple_of(y * nx, nx), nx)
            o_ref[rows, :] = o_ref[rows, :] - jnp.dot(
                c_ref[rows, :], w_ref[...], preferred_element_type=jnp.float32
            )
            return 0

        lax.fori_loop(0, grid_rows, subtract, 0)


def column_step(me, coefs, parts, sources, halo, nx, grid_rows, tile, out_shape, offset,
                own=0, gains=None, into=None):
    width = parts[0].shape[-1]
    steps = width // tile
    lead = offset // tile
    once = pl.Buffered(1)
    specs = [pl.BlockSpec(coefs.shape, lambda j, m: (0, 0, 0), pipeline_mode=once)]
    for part in parts:
        if part.ndim == 3:
            specs.append(
                pl.BlockSpec((None, part.shape[1], tile), lambda j, m: (0, 0, own // tile + j))
            )
        else:
            specs.append(pl.BlockSpec((part.shape[0], tile), lambda j, m: (0, j)))
    args = [coefs, *parts]
    aliases = {}
    if gains is not None:
        c, w = gains
        specs.append(pl.BlockSpec(c.shape, lambda j, m: (0, 0), pipeline_mode=once))
        specs.append(pl.BlockSpec((w.shape[0], tile), lambda j, m: (0, lead + j)))
        args += [c, w]
    if into is not None:
        specs.append(pl.BlockSpec(memory_space=pl.ANY))
        args.append(into)
        aliases = {len(args): 0}
    span = (grid_rows + 4 * REACH) * nx + FRONT + SUB
    scratch = pltpu.VMEM((tile // LANES, span, LANES), jnp.float32)
    return pl.pallas_call(
        functools.partial(
            column_step_kernel, sources=sources, halo=halo, nx=nx, grid_rows=grid_rows,
            update=gains is not None,
        ),
        out_shape=jax.ShapeDtypeStruct(out_shape, jnp.float32),
        grid_spec=pltpu.PrefetchScalarGridSpec(
            num_scalar_prefetch=1,
            grid=(steps,),
            in_specs=specs,
            out_specs=pl.BlockSpec((out_shape[0], tile), lambda j, m: (0, lead + j)),
            scratch_shapes=[scratch, scratch],
        ),
        input_output_aliases=aliases,
        compiler_params=pltpu.CompilerParams(vmem_limit_bytes=60 << 20),
        cost_estimate=work(out_shape[0] * width, 100),
        name="column_step",
    )(me, *args)


def split(value):
    high = lax.reduce_precision(value, 8, 7)
    return high.astype(jnp.bfloat16), (value - high).astype(jnp.bfloat16)


def solve(inner, variance, right):
    system = 0.5 * (inner + inner.T) + jnp.diag(variance)
    factor = jnp.linalg.cholesky(system)
    halfway = lax.linalg.triangular_solve(factor, right, left_side=True, lower=True)
    return lax.linalg.triangular_solve(factor, halfway, left_side=True, lower=True, transpose_a=True)


def gains_of(columns, rows, inner, obs_var):
    updates, count = obs_var.shape
    weights = []
    for u in range(updates):
        here = slice(u * count, (u + 1) * count)
        after = slice((u + 1) * count, updates * count)
        later = inner[here, after]
        both = jnp.concatenate([rows[here], later], axis=1)
        both = solve(inner[here, here], obs_var[u], both)
        w, w_later = both[:, : rows.shape[1]], both[:, rows.shape[1] :]
        weights.append(w)
        if u + 1 < updates:
            left = inner[after, here]
            rows = rows.at[after].add(-jnp.dot(left, w, precision=EXACT))
            columns = columns.at[:, after].add(-jnp.dot(columns[:, here], w_later, precision=EXACT))
            inner = inner.at[after, after].add(-jnp.dot(left, w_later, precision=EXACT))
    c_high, c_low = split(columns)
    w_high, w_low = split(jnp.concatenate(weights, axis=0))
    return (
        jnp.concatenate([c_high, c_high, c_low], axis=1),
        jnp.concatenate([w_high, w_low, w_high], axis=0),
    )


def local(cov_prior, courant_x_field, courant_y_field, obs_cells, obs_var):
    rows, cells = cov_prior.shape
    _, nx = courant_x_field.shape
    members, clusters = lax.axis_size("row"), lax.axis_size("grp")
    zonal, local_rows = cells // members, rows * members
    grid_rows = local_rows // nx
    halo = 2 * REACH * nx
    me, group = lax.axis_index("row"), lax.axis_index("grp")
    me_arg = me.reshape(1).astype(jnp.int32)
    coefs = stencil_coefficients(courant_x_field, courant_y_field)

    per_dest = zonal // nx
    shares, slots = plan(per_dest)
    leads = [sum(shares[:i]) for i in range(len(shares))]
    blocks = []
    row_coefs = coefs[:3] + [courant_x_field / 12.0]
    for lead, depth in zip(leads, shares):
        blocks.append(row_step(cov_prior, row_coefs, me_arg, nx, members, lead, depth))

    column_coefs = jnp.stack(
        [
            jnp.broadcast_to(
                lax.dynamic_slice_in_dim(
                    jnp.pad(c, ((2 * REACH, 2 * REACH), (0, 0))),
                    group * grid_rows, grid_rows + 4 * REACH, 0,
                ).reshape(-1)[:, None],
                (local_rows + 2 * halo, LANES),
            )
            for c in coefs
        ]
    )

    forward = [(i, i + 1) for i in range(clusters - 1)]
    backward = [(i + 1, i) for i in range(clusters - 1)]
    received = []
    for index, start, take in slots:
        cut = slice(start * nx, (start + take) * nx)
        got = [blocks[index][0, :, cut]]
        for s in range(1, members):
            pairs = [(i, i ^ s) for i in range(members)]
            got.append(lax.ppermute(blocks[index][s, :, cut], "row", pairs))
        received.append(got)

    all_cells = obs_cells.reshape(-1)
    picked = pick_columns(blocks, tuple(n * nx for n in leads), all_cells, me, zonal)
    picked = lax.all_gather(picked, "row", axis=0, tiled=True)
    below = lax.ppermute(picked[local_rows - halo :], "grp", forward)
    above = lax.ppermute(picked[:halo], "grp", backward)
    picked = jnp.concatenate([below, picked, above], axis=0)
    count = all_cells.shape[0]
    columns = column_step(
        me_arg, column_coefs, [picked], [("fixed", 0)], halo, nx, grid_rows,
        min(256, count), (local_rows, count), 0,
    )
    first_mine = me * zonal
    mine = lax.dynamic_slice_in_dim(columns, first_mine % local_rows, zonal, 0)
    mine = jnp.where(group == first_mine // local_rows, mine, 0.0)
    place = all_cells - group * local_rows
    held = (place >= 0) & (place < local_rows)
    inner = jnp.where(held[:, None], columns[jnp.clip(place, 0, local_rows - 1)], 0.0)
    mine, inner = lax.psum((mine, inner), "grp")
    gains = gains_of(columns, mine.T, inner, obs_var)

    edge = halo // rows
    result = None
    for k, (index, start, take) in enumerate(slots):
        got = received[k]
        if result is not None:
            got, result = lax.optimization_barrier((got, result))
        last = [lax.select_n(jnp.bitwise_xor(me, members - edge + i), *got) for i in range(edge)]
        head = [lax.select_n(jnp.bitwise_xor(me, i), *got) for i in range(edge)]
        below = lax.ppermute(jnp.concatenate(last, axis=0), "grp", forward)
        above = lax.ppermute(jnp.concatenate(head, axis=0), "grp", backward)
        parts = [below, above, blocks[index]] + got[1:]
        sources = [("fixed", 0), ("fixed", halo + local_rows), ("partner", 0)]
        sources += [("partner", s) for s in range(1, members)]
        result = column_step(
            me_arg, column_coefs, parts, tuple(sources), halo, nx, grid_rows,
            min(256, take * nx), (local_rows, zonal), (leads[index] + start) * nx,
            start * nx, gains, result,
        )
    return result


def plan(per_dest):
    shares = [per_dest] if per_dest <= 4 else [4, per_dest - 4]
    slots = []
    for index, depth in enumerate(shares):
        done = 0
        while done < depth:
            take = min(4, depth - done)
            if index > 0 and depth - done <= 4:
                take = min(2, depth - done)
            slots.append((index, done, take))
            done += take
    return shares, slots


def solution(mesh):
    placed = (P(("grp", "row"), None), P(), P(), P(), P())

    return jax.shard_map(
        local, mesh=mesh, in_specs=placed, out_specs=P("grp", "row"), check_vma=False
    )
```

```python
import functools

import jax
import jax.numpy as jnp
from jax import lax
from jax.experimental import pallas as pl
from jax.experimental.pallas import tpu as pltpu
from jax.sharding import PartitionSpec as P


diffusion = 0.1
LANES = 128
SUB = 8
REACH = 2
EXACT = lax.Precision.HIGHEST


KEEP = 1.0 - 4.0 * diffusion


def difference_matrix(nx):
    gap = lax.broadcasted_iota(jnp.int32, (nx, nx), 0) - lax.broadcasted_iota(jnp.int32, (nx, nx), 1)
    sign = jnp.sign(gap).astype(jnp.float32)
    near, next_near = jnp.abs(gap) == 1, jnp.abs(gap) == 2
    slope = jnp.where(near, 8.0 * sign, jnp.where(next_near, -sign, 0.0))
    around = jnp.where(near, 1.0, jnp.where(gap == 0, KEEP_TENTHS, 0.0))
    once = jnp.concatenate([slope, around], axis=1)
    return jnp.concatenate([once, once], axis=0).astype(jnp.bfloat16)


KEEP_TENTHS = 6.0


def row_step_kernel(
    me_ref, coef_ref, d_ref, p_ref, o_ref, lhs_ref, ds_ref, s_ref, *, nx, per_dest, lead
):
    me = me_ref[0]
    tall = p_ref.shape[0]
    members = o_ref.shape[0]
    depth = o_ref.shape[2] // nx
    zero = jnp.zeros((tall, nx), jnp.float32)

    def at(k):
        return slice((k + 2) * tall, (k + 3) * tall)

    def put(k, value):
        high = value.astype(jnp.bfloat16)
        lhs_ref[at(k), 0:nx] = high
        lhs_ref[at(k), nx : 2 * nx] = (value - high.astype(jnp.float32)).astype(jnp.bfloat16)

    def product(k0, k1):
        rows = slice((k0 + 2) * tall, (k1 + 2) * tall)
        ds_ref[rows, :] = jnp.dot(
            lhs_ref[rows, :], d_ref[...], preferred_element_type=jnp.float32
        )

    def part(dest, low, high):
        y0 = dest * per_dest + lead

        def outside(k):
            return (low and k < 0) or (high and k >= depth)

        def cols(y):
            start = y * nx
            return pl.ds(start if isinstance(start, int) else pl.multiple_of(start, nx), nx)

        def q(k):
            return zero if outside(k) else p_ref[:, cols(y0 + k)]

        def tendency(k, m2, m1, p1, p2):
            c = [coef_ref[i, pl.ds(y0 + k, 1), :] for i in range(4)]
            along_y = (c[0] * p1 + c[1] * m1) + c[2] * (p2 - m2)
            return along_y + (diffusion * ds_ref[at(k), nx : 2 * nx] - c[3] * ds_ref[at(k), 0:nx])

        inside = [k for k in range(-2, depth + 2) if not outside(k)]
        for k in inside:
            put(k, q(k))
        product(inside[0], inside[-1] + 1)
        for k in range(-2, depth + 2):
            if outside(k):
                s_ref[at(k), :] = zero
                continue
            value = tendency(k, q(k - 2), q(k - 1), q(k + 1), q(k + 2))
            s_ref[at(k), :] = value
            if 0 <= k < depth:
                put(k, value)
        product(0, depth)
        slot = jnp.bitwise_xor(jnp.int32(dest), me)
        for k in range(depth):
            value = tendency(
                k, s_ref[at(k - 2), :], s_ref[at(k - 1), :], s_ref[at(k + 1), :], s_ref[at(k + 2), :]
            )
            o_ref[slot, :, k * nx : (k + 1) * nx] = 0.5 * (q(k) + value)

    low, high = lead == 0, lead + depth == per_dest
    if low:
        part(0, True, high and members == 1)

    def one(dest, _):
        part(dest, False, False)
        return 0

    lax.fori_loop(int(low), members - int(high), one, 0)
    if high and not (low and members == 1):
        part(members - 1, False, True)


def row_step(cov, coefs, me, nx, members, lead, depth):
    rows, cells = cov.shape
    per_dest = cells // members // nx
    tall = min(64, rows)
    table = jnp.stack(coefs)
    matrix = difference_matrix(nx)
    once = pl.Buffered(1)
    stack = (depth + 4) * tall
    return pl.pallas_call(
        functools.partial(row_step_kernel, nx=nx, per_dest=per_dest, lead=lead),
        out_shape=jax.ShapeDtypeStruct((members, rows, depth * nx), jnp.float32),
        grid_spec=pltpu.PrefetchScalarGridSpec(
            num_scalar_prefetch=1,
            grid=(rows // tall,),
            in_specs=[
                pl.BlockSpec(table.shape, lambda i, m: (0, 0, 0), pipeline_mode=once),
                pl.BlockSpec(matrix.shape, lambda i, m: (0, 0), pipeline_mode=once),
                pl.BlockSpec((tall, cells), lambda i, m: (i, 0)),
            ],
            out_specs=pl.BlockSpec((members, tall, depth * nx), lambda i, m: (0, i, 0)),
            scratch_shapes=[
                pltpu.VMEM((stack, 2 * nx), jnp.bfloat16),
                pltpu.VMEM((stack, 2 * nx), jnp.float32),
                pltpu.VMEM((stack, nx), jnp.float32),
            ],
        ),
        compiler_params=pltpu.CompilerParams(vmem_limit_bytes=56 << 20),
        cost_estimate=work(members * rows * depth * nx, 60),
        name="row_step",
    )(me, table, matrix, cov)


def work(elements, flops):
    return pl.CostEstimate(
        flops=flops * elements, transcendentals=0, bytes_accessed=32 * elements
    )


def pick_columns(blocks, leads, cells, me, zonal):
    total = 0.0
    for array, lead in zip(blocks, leads):
        members, _, width = array.shape
        for s in range(members):
            first = jnp.bitwise_xor(me, s) * zonal + lead
            ids = first + lax.broadcasted_iota(jnp.int32, (width, cells.shape[0]), 0)
            chosen = (ids == cells[None, :]).astype(jnp.float32)
            total = total + jnp.dot(array[s], chosen, precision=lax.Precision.HIGH)
    return total


FRONT = SUB


def column_step_kernel(me_ref, *refs, sources, halo, nx, grid_rows, update):
    coef_ref, refs = refs[0], refs[1:]
    own = refs[: len(sources)]
    refs = refs[len(sources) :]
    if update:
        c_ref, w_ref = refs[:2]
        refs = refs[2:]
        if len(refs) == 4:
            refs = refs[1:]
    o_ref, q_ref, s_ref = refs
    me = me_ref[0]
    tiles = o_ref.shape[1] // LANES
    stride = nx + SUB
    border = jnp.zeros((SUB, LANES), jnp.float32)
    for t in range(tiles):
        for ref in (q_ref, s_ref):
            for y in range(grid_rows + 4 * REACH + 1):
                ref[t, y * stride : y * stride + SUB, :] = border

    for ref, (kind, at) in zip(own, sources):
        tall = ref.shape[0]
        start = halo + jnp.bitwise_xor(me, at) * tall if kind == "partner" else at
        piece = min(64, tall)

        def copy(i, _):
            r = pl.multiple_of(i * piece, piece)
            cell = start + r
            to = pl.multiple_of(FRONT + cell + (cell // nx) * SUB, SUB)
            for t in range(tiles):
                q_ref[t, pl.ds(to, piece), :] = ref[
                    pl.ds(r, piece), t * LANES : (t + 1) * LANES
                ]
            return 0

        lax.fori_loop(0, tall // piece, copy, 0)

    def sweep(src, low, count, emit):
        def strip(xg, _):
            base = FRONT + xg * SUB

            def at(y, shift=0):
                rows = y * stride + base
                rows = pl.multiple_of(rows, SUB) if shift == 0 else rows + shift
                return [src[t, pl.ds(rows, SUB), :] for t in range(tiles)]

            def step(y, win):
                far = at(y + 2)
                xp1, xm1, xp2, xm2 = at(y, 1), at(y, -1), at(y, 2), at(y, -2)
                spot = pl.multiple_of(y * nx + xg * SUB, SUB)
                u, v = coef_ref[0, pl.ds(spot, SUB), :], coef_ref[1, pl.ds(spot, SUB), :]
                u8, v8 = 8.0 * u, 8.0 * v
                c = (diffusion - v8, diffusion + v8, v, diffusion - u8, diffusion + u8, u)
                for t in range(tiles):
                    along_y = c[0] * win[3][t] + c[1] * win[1][t] + c[2] * (far[t] - win[0][t])
                    along_x = c[3] * xp1[t] + c[4] * xm1[t] + c[5] * (xp2[t] - xm2[t])
                    emit(t, y, xg, KEEP * win[2][t] + (along_y + along_x))
                return win[1:] + [far]

            def several(i, win):
                for k in range(4):
                    win = step(low + 4 * i + k, win)
                return win

            win = [at(low - 2), at(low - 1), at(low), at(low + 1)]
            lax.fori_loop(0, count // 4, several, win)
            return 0

        lax.fori_loop(0, nx // SUB, strip, 0)

    def cell_at(y, xg):
        return pl.ds(pl.multiple_of(y * stride + FRONT + xg * SUB, SUB), SUB)

    def emit_first(t, y, xg, value):
        s_ref[t, cell_at(y, xg), :] = value

    def emit_last(t, y, xg, value):
        row = pl.multiple_of((y - 2 * REACH) * nx + xg * SUB, SUB)
        mid = q_ref[t, cell_at(y, xg), :]
        o_ref[pl.ds(row, SUB), t * LANES : (t + 1) * LANES] = 0.5 * (mid + value)

    sweep(q_ref, REACH, grid_rows + 2 * REACH, emit_first)

    def clear(y0):
        nothing = jnp.zeros((nx, LANES), jnp.float32)
        for t in range(tiles):
            for y in (y0, y0 + 1):
                s_ref[t, y * stride + FRONT : y * stride + FRONT + nx, :] = nothing

    @pl.when(me_ref[1] == 1)
    def _():
        clear(REACH)

    @pl.when(me_ref[2] == 1)
    def _():
        clear(grid_rows + 2 * REACH)

    sweep(s_ref, 2 * REACH, grid_rows, emit_last)

    if update:

        def subtract(y, _):
            rows = pl.ds(pl.multiple_of(y * nx, nx), nx)
            o_ref[rows, :] = o_ref[rows, :] - jnp.dot(
                c_ref[rows, :], w_ref[...], preferred_element_type=jnp.float32
            )
            return 0

        lax.fori_loop(0, grid_rows, subtract, 0)


def column_step(me, coefs, parts, sources, halo, nx, grid_rows, tile, out_shape, offset,
                own=0, gains=None, into=None):
    width = parts[0].shape[-1]
    steps = width // tile
    lead = offset // tile
    once = pl.Buffered(1)
    specs = [pl.BlockSpec(coefs.shape, lambda j, m: (0, 0, 0), pipeline_mode=once)]
    for part in parts:
        if part.ndim == 3:
            specs.append(
                pl.BlockSpec((None, part.shape[1], tile), lambda j, m: (0, 0, own // tile + j))
            )
        else:
            specs.append(pl.BlockSpec((part.shape[0], tile), lambda j, m: (0, j)))
    args = [coefs, *parts]
    aliases = {}
    if gains is not None:
        c, w = gains
        specs.append(pl.BlockSpec(c.shape, lambda j, m: (0, 0), pipeline_mode=once))
        specs.append(pl.BlockSpec((w.shape[0], tile), lambda j, m: (0, lead + j)))
        args += [c, w]
    if into is not None:
        specs.append(pl.BlockSpec(memory_space=pl.ANY))
        args.append(into)
        aliases = {len(args): 0}
    span = (grid_rows + 4 * REACH) * (nx + SUB) + SUB
    scratch = pltpu.VMEM((tile // LANES, span, LANES), jnp.float32)
    return pl.pallas_call(
        functools.partial(
            column_step_kernel, sources=sources, halo=halo, nx=nx, grid_rows=grid_rows,
            update=gains is not None,
        ),
        out_shape=jax.ShapeDtypeStruct(out_shape, jnp.float32),
        grid_spec=pltpu.PrefetchScalarGridSpec(
            num_scalar_prefetch=1,
            grid=(steps,),
            in_specs=specs,
            out_specs=pl.BlockSpec((out_shape[0], tile), lambda j, m: (0, lead + j)),
            scratch_shapes=[scratch, scratch],
        ),
        input_output_aliases=aliases,
        compiler_params=pltpu.CompilerParams(vmem_limit_bytes=60 << 20),
        cost_estimate=work(out_shape[0] * width, 100),
        name="column_step",
    )(me, *args)


def split(value):
    high = lax.reduce_precision(value, 8, 7)
    return high.astype(jnp.bfloat16), (value - high).astype(jnp.bfloat16)


def solve(inner, variance, right):
    system = 0.5 * (inner + inner.T) + jnp.diag(variance)
    factor = jnp.linalg.cholesky(system)
    halfway = lax.linalg.triangular_solve(factor, right, left_side=True, lower=True)
    return lax.linalg.triangular_solve(factor, halfway, left_side=True, lower=True, transpose_a=True)


def gains_of(columns, rows, inner, obs_var):
    updates, count = obs_var.shape
    weights = []
    for u in range(updates):
        here = slice(u * count, (u + 1) * count)
        after = slice((u + 1) * count, updates * count)
        later = inner[here, after]
        both = jnp.concatenate([rows[here], later], axis=1)
        both = solve(inner[here, here], obs_var[u], both)
        w, w_later = both[:, : rows.shape[1]], both[:, rows.shape[1] :]
        weights.append(w)
        if u + 1 < updates:
            left = inner[after, here]
            rows = rows.at[after].add(-jnp.dot(left, w, precision=EXACT))
            columns = columns.at[:, after].add(-jnp.dot(columns[:, here], w_later, precision=EXACT))
            inner = inner.at[after, after].add(-jnp.dot(left, w_later, precision=EXACT))
    c_high, c_low = split(columns)
    w_high, w_low = split(jnp.concatenate(weights, axis=0))
    return (
        jnp.concatenate([c_high, c_high, c_low], axis=1),
        jnp.concatenate([w_high, w_low, w_high], axis=0),
    )


def local(cov_prior, courant_x_field, courant_y_field, obs_cells, obs_var):
    rows, cells = cov_prior.shape
    _, nx = courant_x_field.shape
    members, clusters = lax.axis_size("row"), lax.axis_size("grp")
    zonal, local_rows = cells // members, rows * members
    grid_rows = local_rows // nx
    halo = 2 * REACH * nx
    me, group = lax.axis_index("row"), lax.axis_index("grp")
    ends = (group == 0).astype(jnp.int32), (group == clusters - 1).astype(jnp.int32)
    me_arg = jnp.stack([me.astype(jnp.int32), *ends])

    per_dest = zonal // nx
    shares, slots = plan(per_dest)
    leads = [sum(shares[:i]) for i in range(len(shares))]
    blocks = []
    v12 = courant_y_field / 12.0
    row_coefs = [diffusion - 8.0 * v12, diffusion + 8.0 * v12, v12, courant_x_field / 12.0]
    for lead, depth in zip(leads, shares):
        blocks.append(row_step(cov_prior, row_coefs, me_arg, nx, members, lead, depth))

    column_coefs = jnp.stack(
        [
            jnp.broadcast_to(
                lax.dynamic_slice_in_dim(
                    jnp.pad(c / 12.0, ((2 * REACH, 2 * REACH), (0, 0))),
                    group * grid_rows, grid_rows + 4 * REACH, 0,
                ).reshape(-1)[:, None],
                (local_rows + 2 * halo, LANES),
            )
            for c in (courant_x_field, courant_y_field)
        ]
    )

    forward = [(i, i + 1) for i in range(clusters - 1)]
    backward = [(i + 1, i) for i in range(clusters - 1)]
    received = []
    for index, start, take in slots:
        cut = slice(start * nx, (start + take) * nx)
        got = [blocks[index][0, :, cut]]
        for s in range(1, members):
            pairs = [(i, i ^ s) for i in range(members)]
            got.append(lax.ppermute(blocks[index][s, :, cut], "row", pairs))
        received.append(got)

    all_cells = obs_cells.reshape(-1)
    picked = pick_columns(blocks, tuple(n * nx for n in leads), all_cells, me, zonal)
    picked = lax.all_gather(picked, "row", axis=0, tiled=True)
    below = lax.ppermute(picked[local_rows - halo :], "grp", forward)
    above = lax.ppermute(picked[:halo], "grp", backward)
    picked = jnp.concatenate([below, picked, above], axis=0)
    count = all_cells.shape[0]
    columns = column_step(
        me_arg, column_coefs, [picked], [("fixed", 0)], halo, nx, grid_rows,
        min(256, count), (local_rows, count), 0,
    )
    first_mine = me * zonal
    mine = lax.dynamic_slice_in_dim(columns, first_mine % local_rows, zonal, 0)
    mine = jnp.where(group == first_mine // local_rows, mine, 0.0)
    place = all_cells - group * local_rows
    held = (place >= 0) & (place < local_rows)
    inner = jnp.where(held[:, None], columns[jnp.clip(place, 0, local_rows - 1)], 0.0)
    mine, inner = lax.psum((mine, inner), "grp")
    gains = gains_of(columns, mine.T, inner, obs_var)

    edge = halo // rows

    def edges(got):
        last = [lax.select_n(jnp.bitwise_xor(me, members - edge + i), *got) for i in range(edge)]
        head = [lax.select_n(jnp.bitwise_xor(me, i), *got) for i in range(edge)]
        return jnp.concatenate(last, axis=0), jnp.concatenate(head, axis=0)

    def around(last, head):
        return lax.ppermute(last, "grp", forward), lax.ppermute(head, "grp", backward)

    result = None
    later = around(*edges(received[0]))
    for k, (index, start, take) in enumerate(slots):
        got, (below, above) = received[k], later
        if k + 1 < len(slots):
            if result is None:
                received[k + 1], gains = lax.optimization_barrier((received[k + 1], gains))
            else:
                received[k + 1], result = lax.optimization_barrier((received[k + 1], result))
            below, pair = lax.optimization_barrier((below, edges(received[k + 1])))
            later = around(*pair)
        parts = [below, above, blocks[index]] + got[1:]
        sources = [("fixed", 0), ("fixed", halo + local_rows), ("partner", 0)]
        sources += [("partner", s) for s in range(1, members)]
        result = column_step(
            me_arg, column_coefs, parts, tuple(sources), halo, nx, grid_rows,
            min(256, take * nx), (local_rows, zonal), (leads[index] + start) * nx,
            start * nx, gains, result,
        )
    return result


def plan(per_dest):
    shares = [per_dest] if per_dest <= 4 else [4, per_dest - 4]
    slots = []
    for index, depth in enumerate(shares):
        done = 0
        while done < depth:
            take = min(4, depth - done)
            if index > 0 and depth - done <= 4:
                take = min(2, depth - done)
            slots.append((index, done, take))
            done += take
    return shares, slots


def solution(mesh):
    placed = (P(("grp", "row"), None), P(), P(), P(), P())

    return jax.shard_map(
        local, mesh=mesh, in_specs=placed, out_specs=P("grp", "row"), check_vma=False
    )
```
